256 devices in a mesh: patch: 128 (over z, y, x), slab: 2 (over core).
Axes of the slice: x: 4, y: 4, z: 8, core: 2. Of those that a mesh axis runs over, the one named last changes fastest.
Arguments:
- field: float32 [128, 128, 3, 64, 128], P('patch', 'slab'), may hold values from -6 to 6
- xmats: float32 [128, 2, 64, 64], P('patch'), may hold values from -0.75 to 0.75
- ymats: float32 [128, 2, 128, 128], P('patch'), may hold values from -0.5 to 0.5
- zmats: float32 [128, 2, 128, 128], P('patch'), may hold values from -0.5 to 0.5
- coupling: float32 [128, 3, 3], P('patch'), may hold values from -3.5 to 3.5
- mortar_z: float32 [128, 4, 32, 128], P('patch'), may hold values from -0.5 to 0.5
- mortar_x: float32 [128, 2, 64, 128], P('patch'), may hold values from -0.5 to 0.5
- mortar_y: float32 [128, 2, 64, 64], P('patch'), may hold values from -0.75 to 0.75
- matching: int32 [128, 4], P('patch'), may hold values from 0 to 511, as said below
- orient: int32 [128, 4], P('patch'), may hold values from 0 to 3, as said below
- sizes: int32 [128, 2], P('patch'), may hold values from 32 to 128, as said below
Outputs:
- applied: float32 [128, 128, 3, 64, 128], P('patch', 'slab')
The draws below stay inside these ranges and needn't reach their ends.
Inputs may be any that keep to these rules, and one draw needn't show every extreme that they name: matching[p, f] = 4 q + g says that face f of patch p is glued to face g of patch q; the gluing is symmetric and never joins a face to itself. `orient`: both faces of a gluing carry the same code. sizes[p, 0] lies in 32 to 64, sizes[p, 1] in 64 to 128; some patch has all cells active.
All inputs are finite; a program needn't handle non-finite values.
Results may differ from the reference program's by a relative error of at most 0.0003.
Values sent between devices are 32-bit elements; how exact they have to be, the bound alone decides.
A program may use at most 192 MiB of HBM per device.

```python
import jax
import jax.numpy as jnp
from jax import lax

PATCHES = 128
NX = 64
NY = 128
NZ = 128
MZ = 32
MF = 64


def gluing(key):
    total = 4 * PATCHES
    order = jax.random.permutation(jax.random.fold_in(key, 7), total).astype(jnp.int32)
    first = order[0::2]
    second = order[1::2]
    partner = jnp.zeros((total,), jnp.int32).at[first].set(second).at[second].set(first)
    codes = jax.random.randint(jax.random.fold_in(key, 11), (total // 2,), 0, 4).astype(jnp.int32)
    code_all = jnp.zeros((total,), jnp.int32).at[first].set(codes).at[second].set(codes)
    return (partner.reshape(PATCHES, 4), code_all.reshape(PATCHES, 4))


def draw_matching(key, part):
    return gluing(key)[0]


def draw_orient(key, part):
    return gluing(key)[1]


def draw_sizes(key, part):
    size_x = jax.random.randint(jax.random.fold_in(key, 23), (PATCHES,), NX // 2, NX + 1).astype(jnp.int32)
    size_y = jax.random.randint(jax.random.fold_in(key, 29), (PATCHES,), NY // 2, NY + 1).astype(jnp.int32)
    chosen = jax.random.randint(jax.random.fold_in(key, 31), (), 0, PATCHES)
    size_x = size_x.at[chosen].set(NX)
    size_y = size_y.at[chosen].set(NY)
    return jnp.stack([size_x, size_y], axis=1)


def steps_of(own_key, extent, split, least, top_value):
    level = 1.0
    for dim, shards_of in split:
        steps = jax.random.uniform(jax.random.fold_in(jax.random.fold_in(own_key, 6), dim), (shards_of,), jnp.float32, least / len(split), top_value / len(split))
        level = level * jnp.repeat(jnp.exp(steps), extent[dim] // shards_of).reshape((-1,) + (1,) * (len(extent) - 1 - dim))
    return level


def bell_draw(stream_key, shape, scale, reach, pieces=(), kind=jnp.bfloat16):
    gain = steps_of(stream_key, shape, pieces, -0.22, 0.18) if pieces else 1.0
    values = jax.random.normal(stream_key, shape, jnp.float32) * scale * gain
    return jnp.minimum(jnp.maximum(values, -reach), reach).astype(kind)


def setup_inputs(seed: int = 0) -> dict:
    seeds = jax.random.split(jax.random.key(seed), 12)
    field = bell_draw(seeds[0], (PATCHES, NZ, 3, NX, NY), 1.0, 6.0, ((0, 128), (1, 2)), jnp.float32)
    xmats = bell_draw(seeds[1], (PATCHES, 2, NX, NX), NX ** -0.5, 0.75, ((0, 128),), jnp.float32)
    ymats = bell_draw(seeds[2], (PATCHES, 2, NY, NY), NY ** -0.5, 0.5, ((0, 128),), jnp.float32)
    zmats = bell_draw(seeds[3], (PATCHES, 2, NZ, NZ), NZ ** -0.5, 0.5, ((0, 128),), jnp.float32)
    coupling = bell_draw(seeds[4], (PATCHES, 3, 3), 3 ** -0.5, 3.5, ((0, 128),), jnp.float32)
    mortar_z = bell_draw(seeds[5], (PATCHES, 4, MZ, NZ), NZ ** -0.5, 0.5, ((0, 128),), jnp.float32)
    mortar_x = bell_draw(seeds[6], (PATCHES, 2, MF, NY), NY ** -0.5, 0.5, ((0, 128),), jnp.float32)
    mortar_y = bell_draw(seeds[7], (PATCHES, 2, MF, NX), NX ** -0.5, 0.75, ((0, 128),), jnp.float32)
    matching = draw_matching(jax.random.fold_in(seeds[11], 71), 0)
    orient = draw_orient(jax.random.fold_in(seeds[11], 71), 0)
    sizes = draw_sizes(jax.random.fold_in(seeds[11], 71), 0)
    return dict(field=field, xmats=xmats, ymats=ymats, zmats=zmats, coupling=coupling, mortar_z=mortar_z, mortar_x=mortar_x, mortar_y=mortar_y, matching=matching, orient=orient, sizes=sizes)


highest = lax.Precision.HIGHEST


def plane_masks(size_pair):
    x_index = jnp.arange(NX)
    y_index = jnp.arange(NY)
    active_x = (x_index < size_pair[0]).astype(jnp.float32)
    last_x = (x_index == size_pair[0] - 1).astype(jnp.float32)
    first_x = (x_index == 0).astype(jnp.float32)
    active_y = (y_index < size_pair[1]).astype(jnp.float32)
    last_y = (y_index == size_pair[1] - 1).astype(jnp.float32)
    first_y = (y_index == 0).astype(jnp.float32)
    return active_x, last_x, first_x, active_y, last_y, first_y


def face_project(masked, faces_x, faces_y, mortar_rows, last_x, last_y):
    x_low = masked[:, :, 0, :]
    x_high = jnp.einsum('zcxy,x->zcy', masked, last_x, precision=highest)
    y_low = masked[:, :, :, 0]
    y_high = jnp.einsum('zcxy,y->zcx', masked, last_y, precision=highest)
    along_x = jnp.einsum('fjy,fzcy->fzcj', faces_x, jnp.stack([x_low, x_high]), precision=highest)
    along_y = jnp.einsum('fjx,fzcx->fzcj', faces_y, jnp.stack([y_low, y_high]), precision=highest)
    both = jnp.concatenate([along_x, along_y], axis=0)
    return jnp.einsum('fiz,fzcj->fcij', mortar_rows, both, precision=highest)


def face_spread(jump, faces_x, faces_y, mortar_rows, first_x, last_x, first_y, last_y):
    back_z = jnp.einsum('fiz,fcij->fzcj', mortar_rows, jump, precision=highest)
    back_x = jnp.einsum('fjy,fzcj->fzcy', faces_x, back_z[:2], precision=highest)
    back_y = jnp.einsum('fjx,fzcj->fzcx', faces_y, back_z[2:], precision=highest)
    spread = back_x[0][:, :, None, :] * first_x[None, None, :, None]
    spread = spread + back_x[1][:, :, None, :] * last_x[None, None, :, None]
    spread = spread + back_y[0][:, :, :, None] * first_y[None, None, None, :]
    spread = spread + back_y[1][:, :, :, None] * last_y[None, None, None, :]
    return spread


def flip_codes(near, codes):
    flip_rows = (codes % 2) == 1
    flip_cols = codes >= 2
    near = jnp.where(flip_rows[:, None, None, None], near[:, :, ::-1, :], near)
    return jnp.where(flip_cols[:, None, None, None], near[:, :, :, ::-1], near)


def sum_factor(zstiff, zmass, xmats, ymats):
    first = jnp.einsum('zcxw,yw->zcxy', zmass, ymats[1], precision=highest)
    second = jnp.einsum('zcxw,yw->zcxy', zmass, ymats[0], precision=highest)
    second = second + jnp.einsum('zcxw,yw->zcxy', zstiff, ymats[1], precision=highest)
    result = jnp.einsum('vx,zcxy->zcvy', xmats[0], first, precision=highest)
    return result + jnp.einsum('vx,zcxy->zcvy', xmats[1], second, precision=highest)


def reference(field, xmats, ymats, zmats, coupling, mortar_z, mortar_x, mortar_y, matching, orient, sizes):
    def mortar_one(items):
        block, rows_z, faces_x, faces_y, size_pair = items
        active_x, last_x, first_x, active_y, last_y, first_y = plane_masks(size_pair)
        masked = block * (active_x[:, None] * active_y[None, :])
        return face_project(masked, faces_x, faces_y, rows_z, last_x, last_y)

    mortars = lax.map(mortar_one, (field, mortar_z, mortar_x, mortar_y, sizes))
    partner = matching // 4
    side = matching % 4
    near = mortars[partner, side]
    near = jax.vmap(flip_codes)(near, orient)
    jumps = mortars - near

    def apply_one(items):
        block, mats_x, mats_y, mats_z, mixing, rows_z, faces_x, faces_y, size_pair, jump = items
        active_x, last_x, first_x, active_y, last_y, first_y = plane_masks(size_pair)
        active = active_x[:, None] * active_y[None, :]
        masked = block * active
        mixed = jnp.einsum('cd,zdxy->zcxy', mixing, masked, precision=highest)
        zstiff = jnp.einsum('zw,wcxy->zcxy', mats_z[0], mixed, precision=highest)
        zmass = jnp.einsum('zw,wcxy->zcxy', mats_z[1], mixed, precision=highest)
        inner = sum_factor(zstiff, zmass, mats_x, mats_y)
        spread = face_spread(jump, faces_x, faces_y, rows_z, first_x, last_x, first_y, last_y)
        return (inner + spread) * active

    return lax.map(apply_one, (field, xmats, ymats, zmats, coupling, mortar_z, mortar_x, mortar_y, sizes, jumps))
```

```python
import functools

import jax
import jax.numpy as jnp
from jax import lax
from jax.experimental import pallas as pl
from jax.experimental.pallas import tpu as pltpu
from jax.sharding import PartitionSpec as P

MESH = pl.DeviceIdType.MESH
F32 = jnp.float32
BF16 = jnp.bfloat16
MAT = (((1,), (0,)), ((), ()))
NT = (((1,), (1,)), ((), ()))


def split(a):
    hi = a.astype(BF16)
    return hi, (a - hi.astype(F32)).astype(BF16)


def bdot(a, b, dims=MAT):
    return lax.dot_general(a, b, dims, preferred_element_type=F32)


def dot3(a, b, dims=MAT):
    ah, al = split(a)
    bh, bl = split(b)
    return bdot(ah, bh, dims) + (bdot(ah, bl, dims) + bdot(al, bh, dims))


def rows(ref, start, count, stride):
    return ref[pl.ds(start, count, stride=stride), :]


def face_rows(sizes_ref, mx_ref, my_ref, e_ref):
    e_ref[...] = jnp.zeros((256, 384), F32)
    lane = lax.broadcasted_iota(jnp.int32, (32, 128), 1)
    lane64 = lax.broadcasted_iota(jnp.int32, (32, 64), 1)
    zero = jnp.zeros((32, 64), F32)
    for h in range(2):
        for f in range(2):
            at = h * 128 + f * 32
            j = h * 32
            e_ref[at : at + 32, f * 128 : f * 128 + 128] = jnp.where(
                lane < sizes_ref[0, 1], mx_ref[f, j : j + 32], 0.0
            )
            e = jnp.where(lane64 < sizes_ref[0, 0], my_ref[f, j : j + 32], 0.0)
            e_ref[at + 64 : at + 96, 256:384] = jnp.concatenate(
                [e, zero] if f == 0 else [zero, e], axis=1
            )


def trace_part(sizes_ref, block, t_ref):
    flat = block.reshape(64 * 192, 128)
    sx, sy = sizes_ref[0, 0], sizes_ref[0, 1]
    lane = lax.broadcasted_iota(jnp.int32, (64, 128), 1)
    for d in range(3):

        def body(x, accs):
            low, high = accs
            v = pltpu.roll(rows(flat, d * 64 + x, 64, 192), x, 1)
            low = jnp.where(lane == x, v, low)
            high = jnp.where(lane == lax.rem(x + sy - 1, 128), v, high)
            return low, high

        zero = jnp.zeros((64, 128), F32)
        low, high = lax.fori_loop(0, 64, body, (zero, zero), unroll=8)
        high = pltpu.roll(high, lax.rem(193 - sy, 128), 1)
        at = d * 64
        t_ref[at : at + 64, 0:128] = rows(flat, d * 64, 64, 192)
        t_ref[at : at + 64, 128:256] = rows(flat, d * 64 + jnp.maximum(sx - 1, 0), 64, 192)
        t_ref[at : at + 64, 256:384] = jnp.where(lane < 64, low, high)


def mortar_part(t_ref, s, mz_ref, e_ref):
    along = dot3(t_ref[...], e_ref[...], NT)
    mz = pltpu.roll(mz_ref[...].reshape(128, 128), lax.rem(128 - s * 64, 128), 1)[:, :64]
    face = lax.broadcasted_iota(jnp.int32, (32, 256), 1) % 128 // 32
    parts = []
    for d in range(3):
        full = dot3(mz, along[d * 64 : d * 64 + 64])
        out = jnp.where(face == 0, full[:32], full[32:64])
        out = jnp.where(face == 2, full[64:96], out)
        parts.append(jnp.where(face == 3, full[96:], out))
    return parts


def zy_weights(sizes_ref, s, zm_ref, ym_ref, zl, yw):
    z_rows = [zm_ref[m, pl.ds(pl.multiple_of(s * 64, 64), 64), :] for m in range(2)]
    az = pltpu.roll(jnp.concatenate(z_rows, axis=0), lax.rem(128 - s * 64, 128), 1)
    hi, lo = split(az)
    zl[:128, :128] = hi
    zl[:128, 128:] = hi
    zl[128:, :128] = lo
    zl[128:, 128:] = jnp.zeros_like(lo)
    zero = jnp.zeros((128, 128), BF16)
    sy = sizes_ref[0, 1]
    active = (lax.broadcasted_iota(jnp.int32, (128, 128), 0) < sy) & (
        lax.broadcasted_iota(jnp.int32, (128, 128), 1) < sy
    )
    for k, m in ((0, 1), (256, 0), (512, 1)):
        hi, lo = split(jnp.transpose(jnp.where(active, ym_ref[m], 0.0)))
        yw[k : k + 128, :128] = hi
        yw[k : k + 128, 128:] = lo
        yw[k + 128 : k + 256, :128] = hi
        yw[k + 128 : k + 256, 128:] = zero


def zy_chunk(k, own2, other2, zl, yw, tb, out):
    for pair in range(12):
        tops, lows = [], []
        for n in (2 * pair, 2 * pair + 1):
            start = n // 8 * 64 + n % 8 + k * 8
            top, low = split(
                jnp.concatenate([rows(own2, start, 64, 192), rows(other2, start, 64, 192)], axis=0)
            )
            tops.append(top)
            lows.append(low)
        w = jnp.concatenate(
            [jnp.concatenate(tops, axis=1), jnp.concatenate(lows, axis=1)], axis=0
        )
        r = bdot(zl[...], w)
        t = r[:128] + r[128:]
        for n in range(2):
            at = (2 * pair + n) * 64
            sh, sl = split(t[:64, n * 128 : n * 128 + 128])
            mh, ml = split(t[64:, n * 128 : n * 128 + 128])
            tb[at : at + 64, 0:128] = mh
            tb[at : at + 64, 128:256] = ml
            tb[at : at + 64, 256:384] = sh
            tb[at : at + 64, 384:512] = sl
    for d in range(3):
        at = d * 512
        a = bdot(tb[at : at + 512, :256], yw[:256])
        out[0, d] = (a[:, :128] + a[:, 128:]).reshape(8, 64, 128)
        b = bdot(tb[at : at + 512, :], yw[256:])
        out[1, d] = (b[:, :128] + b[:, 128:]).reshape(8, 64, 128)


def front_kernel(
    sizes_ref, match_ref, field, zm, ym, mz, mx, my, own_ref, near_ref, mid,
    block, other, zm_ref, ym_ref, mz_ref, mx_ref, my_ref, e_ref, t_ref, zl, yw, tb, stage,
    part, got, mine, gath, sendb, mt, mts,
    lsem, wsem, osem, fsem, psem, asem, bsem, csem, dsem,
):
    p = lax.axis_index("patch")
    s = lax.axis_index("slab")
    z, y, x = p // 16, p // 4 % 4, p % 4
    me = z * 4 + x

    def dev(a, yy):
        return (a // 4 * 16 + yy * 4 + a % 4, s)

    partner = (p, 1 - s)

    def copy(src, dst, sem, k, where):
        return pltpu.make_async_remote_copy(
            src, dst, sem.at[0, k], sem.at[1, k], device_id=where, device_id_type=MESH
        )

    barrier = pltpu.get_barrier_semaphore()

    def greet(d, c):
        pl.semaphore_signal(
            barrier, inc=1, device_id=dev((me + d) % 32, y), device_id_type=MESH
        )
        return c

    pl.semaphore_signal(barrier, inc=1, device_id=partner, device_id_type=MESH)
    lax.fori_loop(1, 32, greet, 0)

    def greet_y(d, c):
        pl.semaphore_signal(
            barrier, inc=1, device_id=dev(me, (y + d) % 4), device_id_type=MESH
        )
        return c

    lax.fori_loop(1, 4, greet_y, 0)

    load = pltpu.make_async_copy(field.at[0], block, lsem.at[0])
    load.start()
    smalls = [
        pltpu.make_async_copy(a.at[0], b, wsem.at[n])
        for n, (a, b) in enumerate(
            ((zm, zm_ref), (ym, ym_ref), (mz, mz_ref), (mx, mx_ref), (my, my_ref))
        )
    ]
    for c in smalls:
        c.start()
    for c in smalls:
        c.wait()
    face_rows(sizes_ref, mx_ref, my_ref, e_ref)
    zy_weights(sizes_ref, s, zm_ref, ym_ref, zl, yw)
    lane1 = lax.broadcasted_iota(jnp.int32, (1, 128), 1)
    row = jnp.where(lane1 == 0, match_ref[0, 0], match_ref[0, 1])
    row = jnp.where(lane1 == 2, match_ref[0, 2], row)
    mt[me] = jnp.where(lane1 == 3, match_ref[0, 3], row)
    load.wait()
    trace_part(sizes_ref, block, t_ref)
    pl.semaphore_wait(barrier, 35)

    def field_copy(k):
        at = pl.ds(pl.multiple_of(k * 8, 8), 8)
        return copy(field.at[0, :, :, at], other.at[:, :, at], fsem, k, partner)

    def start_field(k, c):
        field_copy(k).start()
        return c

    lax.fori_loop(0, 8, start_field, 0)

    def match_copy(d):
        return copy(mt.at[me], mt.at[me], asem, d, dev((me + d) % 32, y))

    def start_match(d, c):
        match_copy(d).start()
        return c

    lax.fori_loop(1, 32, start_match, 0)

    parts = mortar_part(t_ref, s, mz_ref, e_ref)
    half = s == 0
    for d in range(3):
        part[d] = jnp.where(half, parts[d][:, 128:], parts[d][:, :128])
    c0 = copy(part, got, psem, 0, partner)
    c0.start()
    for d in range(3):
        mine[:, d, :] = jnp.where(half, parts[d][:, :128], parts[d][:, 128:])
    mine[:, 3, :] = jnp.zeros((32, 128), F32)

    own2 = block.reshape(64 * 192, 128)
    other2 = other.reshape(64 * 192, 128)

    def mid_copy(k):
        at = pl.ds(pl.multiple_of(k * 8, 8), 8)
        return pltpu.make_async_copy(stage.at[k % 2], mid.at[:, :, at], osem.at[k % 2])

    def chunks(lo, hi):
        def one(k, c):
            field_copy(k).wait()

            @pl.when(k >= 2)
            def _():
                mid_copy(k - 2).wait()

            zy_chunk(k, own2, other2, zl, yw, tb, stage.at[k % 2])
            mid_copy(k).start()
            return c

        lax.fori_loop(lo, hi, one, 0)

    chunks(0, CUTS[0])
    c0.wait()
    for d in range(3):
        mine[:, d, :] = mine[:, d, :] + got[d]

    def spread_copy(d):
        a = (me + d) % 32
        return copy(mine.at[a], gath.at[y, me], bsem, d, dev(a, y))

    def start_spread(d, c):
        spread_copy(d).start()
        return c

    lax.fori_loop(1, 32, start_spread, 0)
    cm = copy(mine, own_ref.at[s], psem, 1, partner)
    cm.start()
    own_ref[s] = mine[...]
    gath[y, me] = mine[me]

    def wait_match(d, c):
        match_copy(d).wait()
        return c

    lax.fori_loop(1, 32, wait_match, 0)
    tos = pltpu.make_async_copy(mt, mts, lsem.at[1])
    tos.start()
    chunks(CUTS[0], CUTS[1])

    def wait_spread(d, c):
        spread_copy(d).wait()
        return c

    lax.fori_loop(1, 32, wait_spread, 0)

    def line_copy(d):
        return copy(gath.at[y], gath.at[y], csem, d, dev(me, (y + d) % 4))

    for d in range(1, 4):
        line_copy(d).start()
    tos.wait()
    chunks(CUTS[1], CUTS[2])
    for d in range(1, 4):
        line_copy(d).wait()

    lane4 = lax.broadcasted_iota(jnp.int32, (4, 128), 1) // 32

    def pick(a, c):
        out = jnp.zeros((4, 128), F32)
        for f in range(4):
            m = mts[a, 0, f]
            q = m // 4
            v = gath[q // 4 % 4, q // 16 * 4 + q % 4]
            v = pltpu.roll(v, (f + 4 - m % 4) % 4 * 32, 1)
            out = jnp.where(lane4 == f, v, out)
        sendb[a] = out
        return c

    lax.fori_loop(0, 32, pick, 0, unroll=4)

    def back_copy(d):
        a = (me + d) % 32
        return copy(sendb.at[a], near_ref.at[s, me], dsem, d, dev(a, y))

    def start_back(d, c):
        back_copy(d).start()
        return c

    lax.fori_loop(1, 32, start_back, 0)
    near_ref[s, me] = sendb[me]
    chunks(CUTS[2], 8)

    def wait_back(d, c):
        back_copy(d).wait()
        return c

    lax.fori_loop(1, 32, wait_back, 0)
    cn = copy(near_ref.at[s], near_ref.at[s], psem, 2, partner)
    cn.start()
    cm.wait()
    mid_copy(6).wait()
    mid_copy(7).wait()
    cn.wait()


CUTS = (1, 4, 6)


def front(sizes, matching, field, zm, ym, mz, mx, my):
    vmem = pl.BlockSpec(memory_space=pltpu.VMEM)
    smem = pl.BlockSpec(memory_space=pltpu.SMEM)
    hbm = pl.BlockSpec(memory_space=pl.ANY)
    dma = pltpu.SemaphoreType.DMA
    shape = jax.ShapeDtypeStruct((2, 32, 4, 128), F32)
    return pl.pallas_call(
        front_kernel,
        out_shape=(shape, shape, jax.ShapeDtypeStruct((2, 3, 64, 64, 128), F32)),
        in_specs=[smem, smem] + [hbm] * 6,
        out_specs=(vmem, vmem, hbm),
        scratch_shapes=[
            pltpu.VMEM((64, 3, 64, 128), F32),
            pltpu.VMEM((64, 3, 64, 128), F32),
            pltpu.VMEM((2, 128, 128), F32),
            pltpu.VMEM((2, 128, 128), F32),
            pltpu.VMEM((4, 32, 128), F32),
            pltpu.VMEM((2, 64, 128), F32),
            pltpu.VMEM((2, 64, 64), F32),
            pltpu.VMEM((256, 384), F32),
            pltpu.VMEM((192, 384), F32),
            pltpu.VMEM((256, 256), BF16),
            pltpu.VMEM((768, 256), BF16),
            pltpu.VMEM((1536, 512), BF16),
            pltpu.VMEM((2, 2, 3, 8, 64, 128), F32),
            pltpu.VMEM((3, 32, 128), F32),
            pltpu.VMEM((3, 32, 128), F32),
            pltpu.VMEM((32, 4, 128), F32),
            pltpu.VMEM((4, 32, 4, 128), F32),
            pltpu.VMEM((32, 4, 128), F32),
            pltpu.VMEM((32, 1, 128), jnp.int32),
            pltpu.SMEM((32, 1, 128), jnp.int32),
            dma((2,)), dma((5,)), dma((2,)), dma((2, 8)), dma((2, 3)),
            dma((2, 32)), dma((2, 32)), dma((2, 4)), dma((2, 32)),
        ],
        compiler_params=pltpu.CompilerParams(
            collective_id=0, has_side_effects=True, vmem_limit_bytes=60 * 2**20
        ),
        name="front",
    )(sizes, matching, field, zm, ym, mz, mx, my)


def turned(size, low, mask, flags):
    r = lax.broadcasted_iota(jnp.int32, (size, size), 0)
    c = lax.broadcasted_iota(jnp.int32, (size, size), 1)
    face = r // 32 % 4
    flag = jnp.where(face == 0, flags[0], flags[1])
    flag = jnp.where(face == 2, flags[2], flag)
    flag = jnp.where(face == 3, flags[3], flag)
    return jnp.where(c == (r ^ jnp.where(flag == 1, mask, 0)), 1.0, 0.0).astype(BF16)


def back_part(orient_ref, own_ref, near_ref, mz_ref, e_ref, s, bx, by):
    codes = [orient_ref[0, f] for f in range(4)]
    face = lax.broadcasted_iota(jnp.int32, (32, 128), 1) // 32
    own2 = own_ref.reshape(256, 128)
    near2 = near_ref.reshape(256, 128)
    mz = pltpu.roll(mz_ref[...].reshape(128, 128), lax.rem(128 - s * 64, 128), 1)
    zh, zlo = split(jnp.transpose(mz)[:64])
    perm = turned(128, 5, 31, [c % 2 for c in codes])
    mats = (
        (own2, zh, zlo),
        (near2, bdot(zh, perm).astype(BF16), bdot(zlo, perm).astype(BF16)),
    )
    cols = []
    for data, mh, ml in mats:
        for h in range(2):
            per = []
            for c in range(3):
                v = rows(data, h * 128 + c, 32, 4)
                wide = jnp.concatenate(
                    [jnp.where(face == f, v, 0.0) for f in range(4)], axis=0
                )
                wh, wl = split(wide)
                per.append(bdot(mh, wh) + (bdot(ml, wh) + bdot(mh, wl)))
            cols.append(jnp.concatenate(per, axis=0))
    ch, cl = split(jnp.concatenate(cols, axis=1))
    eh, el = split(e_ref[...])
    perm = turned(256, 5, 159, [c // 2 for c in codes])
    eh = jnp.concatenate([eh, (-bdot(perm, eh)).astype(BF16)], axis=0)
    el = jnp.concatenate([el, (-bdot(perm, el)).astype(BF16)], axis=0)
    back = bdot(ch, eh) + (bdot(ch, el) + bdot(cl, eh))
    for c in range(3):
        r = back[c * 64 : c * 64 + 64]
        bx[0, c] = r[:, :128]
        bx[1, c] = r[:, 128:256]
        col = r[:, 256:]
        by[c] = jnp.transpose(jnp.concatenate([col, col], axis=0))


def last_kernel(
    sizes_ref, cpl, orient_ref, data, xm_ref, own_ref, near_ref, mz_ref, mx_ref, my_ref, out,
    xl, e_ref, bx, by,
):
    i = pl.program_id(0)
    sx, sy = sizes_ref[0, 0], sizes_ref[0, 1]

    @pl.when(i == 0)
    def _():
        active = (lax.broadcasted_iota(jnp.int32, (64, 64), 0) < sx) & (
            lax.broadcasted_iota(jnp.int32, (64, 64), 1) < sx
        )
        h0, l0 = split(jnp.where(active, xm_ref[0], 0.0))
        h1, l1 = split(jnp.where(active, xm_ref[1], 0.0))
        hi = jnp.concatenate([h0, h1], axis=1)
        xl[:64, :128] = hi
        xl[:64, 128:] = hi
        xl[64:, :128] = jnp.concatenate([l0, l1], axis=1)
        xl[64:, 128:] = jnp.zeros((64, 128), BF16)
        face_rows(sizes_ref, mx_ref, my_ref, e_ref)
        back_part(orient_ref, own_ref, near_ref, mz_ref, e_ref, lax.axis_index("slab"), bx, by)

    row = lax.broadcasted_iota(jnp.int32, (64, 128), 0)
    lane = lax.broadcasted_iota(jnp.int32, (64, 128), 1)
    first_x = row == 0
    last_x = row == sx - 1
    first_y = lane == 0
    last_y = lane == sy - 1
    flat = data.reshape(2 * 3 * 64 * 8, 128)
    cols = [pltpu.roll(by[c], lax.rem(128 - i * 8, 128), 1) for c in range(3)]
    for pair in range(4):
        inner = []
        for d in range(3):
            tops, lows = [], []
            for n in range(2):
                k = pair * 2 + n
                first = rows(flat, d * 512 + k, 64, 8)
                second = rows(flat, 1536 + d * 512 + k, 64, 8)
                top, low = split(jnp.concatenate([first, second], axis=0))
                tops.append(top)
                lows.append(low)
            w = jnp.concatenate(
                [jnp.concatenate(tops, axis=1), jnp.concatenate(lows, axis=1)], axis=0
            )
            r = bdot(xl[...], w)
            inner.append(r[:64] + r[64:])
        for c in range(3):
            mix = cpl[0, c, 0] * inner[0] + cpl[0, c, 1] * inner[1] + cpl[0, c, 2] * inner[2]
            for n in range(2):
                k = pair * 2 + n
                v = mix[:, n * 128 : n * 128 + 128]
                zrow = pl.ds(i * 8 + k, 1)
                v = v + jnp.where(first_x, bx[0, c, zrow, :], 0.0)
                v = v + jnp.where(last_x, bx[1, c, zrow, :], 0.0)
                v = v + jnp.where(first_y, cols[c][:64, k : k + 1], 0.0)
                v = v + jnp.where(last_y, cols[c][64:, k : k + 1], 0.0)
                out[k, c] = v


def first_spread(sizes, cpl, orient, data, xm, own, near, mz, mx, my):
    smem = pl.BlockSpec(memory_space=pltpu.SMEM)
    whole = lambda *shape: pl.BlockSpec(shape, lambda i: (0,) * len(shape))
    return pl.pallas_call(
        last_kernel,
        grid=(8,),
        out_shape=jax.ShapeDtypeStruct((1, 64, 3, 64, 128), F32),
        in_specs=[
            smem,
            smem,
            smem,
            pl.BlockSpec((2, 3, 64, 8, 128), lambda i: (0, 0, 0, i, 0)),
            whole(None, 2, 64, 64),
            whole(2, 32, 4, 128),
            whole(2, 32, 4, 128),
            whole(None, 4, 32, 128),
            whole(None, 2, 64, 128),
            whole(None, 2, 64, 64),
        ],
        out_specs=pl.BlockSpec((None, 8, 3, 64, 128), lambda i: (0, i, 0, 0, 0)),
        scratch_shapes=[
            pltpu.VMEM((128, 256), BF16),
            pltpu.VMEM((256, 384), F32),
            pltpu.VMEM((2, 3, 64, 128), F32),
            pltpu.VMEM((3, 128, 128), F32),
        ],
        compiler_params=pltpu.CompilerParams(vmem_limit_bytes=60 * 2**20),
        name="first_spread",
    )(sizes, cpl, orient, data, xm, own, near, mz, mx, my)


def per_device(
    field, xmats, ymats, zmats, coupling, mortar_z, mortar_x, mortar_y, matching, orient, sizes
):
    own, near, mid = front(sizes, matching, field, zmats, ymats, mortar_z, mortar_x, mortar_y)
    return first_spread(
        sizes, coupling, orient, mid, xmats, own, near, mortar_z, mortar_x, mortar_y
    )


def solution(mesh):
    in_specs = (
        P("patch", "slab", None, None, None),
        P("patch", None, None, None),
        P("patch", None, None, None),
        P("patch", None, None, None),
        P("patch", None, None),
        P("patch", None, None, None),
        P("patch", None, None, None),
        P("patch", None, None, None),
        P("patch", None),
        P("patch", None),
        P("patch", None),
    )
    return jax.shard_map(
        per_device,
        mesh=mesh,
        in_specs=in_specs,
        out_specs=P("patch", "slab", None, None, None),
        check_vma=False,
    )
```

```python
import functools

import jax
import jax.numpy as jnp
from jax import lax
from jax.experimental import pallas as pl
from jax.experimental.pallas import tpu as pltpu
from jax.sharding import PartitionSpec as P

MESH = pl.DeviceIdType.MESH
F32 = jnp.float32
BF16 = jnp.bfloat16
MAT = (((1,), (0,)), ((), ()))
NT = (((1,), (1,)), ((), ()))


def split(a):
    hi = a.astype(BF16)
    return hi, (a - hi.astype(F32)).astype(BF16)


def bdot(a, b, dims=MAT):
    return lax.dot_general(a, b, dims, preferred_element_type=F32)


def dot3(a, b, dims=MAT):
    ah, al = split(a)
    bh, bl = split(b)
    return bdot(ah, bh, dims) + (bdot(ah, bl, dims) + bdot(al, bh, dims))


def rows(ref, start, count, stride):
    return ref[pl.ds(start, count, stride=stride), :]


def face_rows(sizes_ref, mx_ref, my_ref, e_ref):
    e_ref[...] = jnp.zeros((256, 384), F32)
    lane = lax.broadcasted_iota(jnp.int32, (32, 128), 1)
    lane64 = lax.broadcasted_iota(jnp.int32, (32, 64), 1)
    zero = jnp.zeros((32, 64), F32)
    for h in range(2):
        for f in range(2):
            at = h * 128 + f * 32
            j = h * 32
            e_ref[at : at + 32, f * 128 : f * 128 + 128] = jnp.where(
                lane < sizes_ref[0, 1], mx_ref[f, j : j + 32], 0.0
            )
            e = jnp.where(lane64 < sizes_ref[0, 0], my_ref[f, j : j + 32], 0.0)
            e_ref[at + 64 : at + 96, 256:384] = jnp.concatenate(
                [e, zero] if f == 0 else [zero, e], axis=1
            )


def trace_part(sizes_ref, block, t_ref):
    sx, sy = sizes_ref[0, 0], sizes_ref[0, 1]
    lane = lax.broadcasted_iota(jnp.int32, (64, 128), 1)
    for d in range(3):

        def body(x, accs):
            low, high = accs
            v = pltpu.roll(block[d, x], x, 1)
            low = jnp.where(lane == x, v, low)
            high = jnp.where(lane == lax.rem(x + sy - 1, 128), v, high)
            return low, high

        zero = jnp.zeros((64, 128), F32)
        low, high = lax.fori_loop(0, 64, body, (zero, zero), unroll=8)
        high = pltpu.roll(high, lax.rem(193 - sy, 128), 1)
        at = d * 64
        t_ref[at : at + 64, 0:128] = block[d, 0]
        t_ref[at : at + 64, 128:256] = block[d, jnp.maximum(sx - 1, 0)]
        t_ref[at : at + 64, 256:384] = jnp.where(lane < 64, low, high)


def mortar_part(t_ref, s, mz_ref, e_ref):
    along = dot3(t_ref[...], e_ref[...], NT)
    mz = pltpu.roll(mz_ref[...].reshape(128, 128), lax.rem(128 - s * 64, 128), 1)[:, :64]
    face = lax.broadcasted_iota(jnp.int32, (32, 256), 1) % 128 // 32
    parts = []
    for d in range(3):
        full = dot3(mz, along[d * 64 : d * 64 + 64])
        out = jnp.where(face == 0, full[:32], full[32:64])
        out = jnp.where(face == 2, full[64:96], out)
        parts.append(jnp.where(face == 3, full[96:], out))
    return parts


def zy_weights(sizes_ref, s, zm_ref, ym_ref, zl, yw):
    z_rows = [zm_ref[m, pl.ds(pl.multiple_of(s * 64, 64), 64), :] for m in range(2)]
    az = pltpu.roll(jnp.concatenate(z_rows, axis=0), lax.rem(128 - s * 64, 128), 1)
    hi, lo = split(az)
    zl[:128, :128] = hi
    zl[:128, 128:] = hi
    zl[128:, :128] = lo
    zl[128:, 128:] = jnp.zeros_like(lo)
    zero = jnp.zeros((128, 128), BF16)
    sy = sizes_ref[0, 1]
    active = (lax.broadcasted_iota(jnp.int32, (128, 128), 0) < sy) & (
        lax.broadcasted_iota(jnp.int32, (128, 128), 1) < sy
    )
    for k, m in ((0, 1), (256, 0), (512, 1)):
        hi, lo = split(jnp.transpose(jnp.where(active, ym_ref[m], 0.0)))
        yw[k : k + 128, :128] = hi
        yw[k : k + 128, 128:] = lo
        yw[k + 128 : k + 256, :128] = hi
        yw[k + 128 : k + 256, 128:] = zero


def zy_chunk(k, own, other, zl, yw, tb, out):
    for pair in range(12):
        tops, lows = [], []
        for n in (2 * pair, 2 * pair + 1):
            at = (n // 8, n % 8 + k * 8)
            top, low = split(
                jnp.concatenate([own[at], other[at]], axis=0)
            )
            tops.append(top)
            lows.append(low)
        w = jnp.concatenate(
            [jnp.concatenate(tops, axis=1), jnp.concatenate(lows, axis=1)], axis=0
        )
        r = bdot(zl[...], w)
        t = r[:128] + r[128:]
        for n in range(2):
            at = (2 * pair + n) * 64
            sh, sl = split(t[:64, n * 128 : n * 128 + 128])
            mh, ml = split(t[64:, n * 128 : n * 128 + 128])
            tb[at : at + 64, 0:128] = mh
            tb[at : at + 64, 128:256] = ml
            tb[at : at + 64, 256:384] = sh
            tb[at : at + 64, 384:512] = sl
    for d in range(3):
        at = d * 512
        a = bdot(tb[at : at + 512, :256], yw[:256])
        out[0, d] = (a[:, :128] + a[:, 128:]).reshape(8, 64, 128)
        b = bdot(tb[at : at + 512, :], yw[256:])
        out[1, d] = (b[:, :128] + b[:, 128:]).reshape(8, 64, 128)


def front_kernel(
    sizes_ref, match_ref, field, zm, ym, mz, mx, my, own_ref, near_ref, mid,
    block, other, zm_ref, ym_ref, mz_ref, mx_ref, my_ref, e_ref, t_ref, zl, yw, tb, stage,
    part, got, mine, gath, sendb, mt, mts,
    lsem, wsem, osem, fsem, psem, asem, bsem, csem, dsem,
):
    p = lax.axis_index("patch")
    s = lax.axis_index("slab")
    z, y, x = p // 16, p // 4 % 4, p % 4
    me = z * 4 + x

    def dev(a, yy):
        return ((a >> 2) * 16 + yy * 4 + (a & 3), s)

    partner = (p, 1 - s)

    def copy(src, dst, sem, k, where):
        return pltpu.make_async_remote_copy(
            src, dst, sem.at[0, k], sem.at[1, k], device_id=where, device_id_type=MESH
        )

    barrier = pltpu.get_barrier_semaphore()

    def greet(d, c):
        pl.semaphore_signal(
            barrier, inc=1, device_id=dev((me + d) & 31, y), device_id_type=MESH
        )
        return c

    pl.semaphore_signal(barrier, inc=1, device_id=partner, device_id_type=MESH)
    lax.fori_loop(1, 32, greet, 0)

    def greet_y(d, c):
        pl.semaphore_signal(
            barrier, inc=1, device_id=dev(me, (y + d) % 4), device_id_type=MESH
        )
        return c

    lax.fori_loop(1, 4, greet_y, 0)

    smalls = [
        pltpu.make_async_copy(a.at[0], b, wsem.at[n])
        for n, (a, b) in enumerate(
            ((mz, mz_ref), (mx, mx_ref), (my, my_ref), (zm, zm_ref), (ym, ym_ref))
        )
    ]
    for c in smalls:
        c.start()
    for d in range(3):

        def load_row(x, c):
            pltpu.make_async_copy(
                field.at[0, :, d, x, 0], block.at[d, x], lsem.at[d]
            ).start()
            return c

        lax.fori_loop(0, 64, load_row, 0, unroll=4)
    for c in smalls[:3]:
        c.wait()
    face_rows(sizes_ref, mx_ref, my_ref, e_ref)
    lane1 = lax.broadcasted_iota(jnp.int32, (1, 128), 1)
    row = jnp.where(lane1 == 0, match_ref[0, 0], match_ref[0, 1])
    row = jnp.where(lane1 == 2, match_ref[0, 2], row)
    row = jnp.where(lane1 == 3, match_ref[0, 3], row)
    q = row >> 2
    mt[me] = ((((q >> 2) & 3) * 32 + (q >> 4) * 4 + (q & 3)) << 2) + (row & 3)
    for d in range(3):
        pltpu.make_async_copy(block.at[d], block.at[d], lsem.at[d]).wait()
    trace_part(sizes_ref, block, t_ref)
    parts = mortar_part(t_ref, s, mz_ref, e_ref)
    half = s == 0
    for d in range(3):
        part[d] = jnp.where(half, parts[d][:, 128:], parts[d][:, :128])
    for d in range(3):
        mine[:, d, :] = jnp.where(half, parts[d][:, :128], parts[d][:, 128:])
    mine[:, 3, :] = jnp.zeros((32, 128), F32)
    pl.semaphore_wait(barrier, 35)
    c0 = copy(part, got, psem, 0, partner)
    c0.start()

    def field_start(k, c):
        for d in range(3):
            for n in range(8):
                x = k * 8 + n
                copy(field.at[0, :, d, x, 0], other.at[d, x], fsem, k, partner).start()
        return c

    def field_wait(k):
        at = other.at[:, pl.ds(pl.multiple_of(k * 8, 8), 8)]
        copy(at, at, fsem, k, partner).wait()

    def match_copy(d):
        return copy(mt.at[me], mt.at[me], asem, d, dev((me + d) & 31, y))

    def start_match(d, c):
        match_copy(d).start()
        return c

    lax.fori_loop(1, 32, start_match, 0)
    field_start(0, 0)


    def mid_start(k):
        for m in range(2):
            for d in range(3):
                for n in range(8):
                    pltpu.make_async_copy(
                        stage.at[k % 2, m, d, n], mid.at[m, d, :, k * 8 + n, 0], osem.at[k % 2]
                    ).start()

    def mid_wait(k):
        pltpu.make_async_copy(stage.at[k % 2], stage.at[k % 2], osem.at[k % 2]).wait()

    def chunks(lo, hi):
        def one(k, c):
            field_wait(k)

            @pl.when(k >= 2)
            def _():
                mid_wait(k - 2)

            zy_chunk(k, block, other, zl, yw, tb, stage.at[k % 2])
            mid_start(k)
            return c

        lax.fori_loop(lo, hi, one, 0)

    c0.wait()
    for d in range(3):
        mine[:, d, :] = mine[:, d, :] + got[d]

    def spread_copy(d):
        a = (me + d) & 31
        return copy(mine.at[a], gath.at[y * 32 + me], bsem, d, dev(a, y))

    def start_spread(d, c):
        spread_copy(d).start()
        return c

    lax.fori_loop(1, 32, start_spread, 0)
    lax.fori_loop(1, 8, field_start, 0)
    cm = copy(mine, own_ref.at[s], psem, 1, partner)
    cm.start()
    own_ref[s] = mine[...]
    gath[y * 32 + me] = mine[me]

    def wait_match(d, c):
        match_copy(d).wait()
        return c

    lax.fori_loop(1, 32, wait_match, 0)
    tos = pltpu.make_async_copy(mt, mts, lsem.at[3])
    tos.start()
    for c in smalls[3:]:
        c.wait()
    zy_weights(sizes_ref, s, zm_ref, ym_ref, zl, yw)
    chunks(0, CUTS[1])

    def wait_spread(d, c):
        spread_copy(d).wait()
        return c

    lax.fori_loop(1, 32, wait_spread, 0)

    def line_copy(d):
        at = gath.at[pl.ds(pl.multiple_of(y * 32, 32), 32)]
        return copy(at, at, csem, d, dev(me, (y + d) % 4))

    for d in range(1, 4):
        line_copy(d).start()
    tos.wait()
    chunks(CUTS[1], CUTS[2])
    for d in range(1, 4):
        line_copy(d).wait()

    lane4 = lax.broadcasted_iota(jnp.int32, (4, 128), 1) // 32

    def pick(d, c):
        a = (me + d) & 31
        out = jnp.zeros((4, 128), F32)
        for f in range(4):
            m = mts[a, 0, f]
            v = pltpu.roll(gath[m >> 2], ((f - m) & 3) * 32, 1)
            out = jnp.where(lane4 == f, v, out)
        sendb[a] = out
        return c

    def back_copy(d):
        a = (me + d) & 31
        return copy(sendb.at[a], near_ref.at[s, me], dsem, d, dev(a, y))

    def start_back(d, c):
        back_copy(d).start()
        return c

    lax.fori_loop(1, 17, pick, 0, unroll=8)
    lax.fori_loop(17, 33, pick, 0, unroll=8)
    lax.fori_loop(1, 32, start_back, 0)
    near_ref[s, me] = sendb[me]
    chunks(CUTS[2], 8)

    def wait_back(d, c):
        back_copy(d).wait()
        return c

    lax.fori_loop(1, 32, wait_back, 0)
    cn = copy(near_ref.at[s], near_ref.at[s], psem, 2, partner)
    cn.start()
    cm.wait()
    mid_wait(6)
    mid_wait(7)
    cn.wait()


CUTS = (0, 3, 6)


def front(sizes, matching, field, zm, ym, mz, mx, my):
    vmem = pl.BlockSpec(memory_space=pltpu.VMEM)
    smem = pl.BlockSpec(memory_space=pltpu.SMEM)
    hbm = pl.BlockSpec(memory_space=pl.ANY)
    dma = pltpu.SemaphoreType.DMA
    shape = jax.ShapeDtypeStruct((2, 32, 4, 128), F32)
    return pl.pallas_call(
        front_kernel,
        out_shape=(shape, shape, jax.ShapeDtypeStruct((2, 3, 64, 64, 1, 128), F32)),
        in_specs=[smem, smem] + [hbm] * 6,
        out_specs=(vmem, vmem, hbm),
        scratch_shapes=[
            pltpu.VMEM((3, 64, 64, 128), F32),
            pltpu.VMEM((3, 64, 64, 128), F32),
            pltpu.VMEM((2, 128, 128), F32),
            pltpu.VMEM((2, 128, 128), F32),
            pltpu.VMEM((4, 32, 128), F32),
            pltpu.VMEM((2, 64, 128), F32),
            pltpu.VMEM((2, 64, 64), F32),
            pltpu.VMEM((256, 384), F32),
            pltpu.VMEM((192, 384), F32),
            pltpu.VMEM((256, 256), BF16),
            pltpu.VMEM((768, 256), BF16),
            pltpu.VMEM((1536, 512), BF16),
            pltpu.VMEM((2, 2, 3, 8, 64, 128), F32),
            pltpu.VMEM((3, 32, 128), F32),
            pltpu.VMEM((3, 32, 128), F32),
            pltpu.VMEM((32, 4, 128), F32),
            pltpu.VMEM((128, 4, 128), F32),
            pltpu.VMEM((32, 4, 128), F32),
            pltpu.VMEM((32, 1, 128), jnp.int32),
            pltpu.SMEM((32, 1, 128), jnp.int32),
            dma((4,)), dma((5,)), dma((2,)), dma((2, 8)), dma((2, 3)),
            dma((2, 32)), dma((2, 32)), dma((2, 4)), dma((2, 32)),
        ],
        compiler_params=pltpu.CompilerParams(
            collective_id=0, has_side_effects=True, vmem_limit_bytes=60 * 2**20
        ),
        name="front",
    )(sizes, matching, field, zm, ym, mz, mx, my)


def turned(size, low, mask, flags):
    r = lax.broadcasted_iota(jnp.int32, (size, size), 0)
    c = lax.broadcasted_iota(jnp.int32, (size, size), 1)
    face = r // 32 % 4
    flag = jnp.where(face == 0, flags[0], flags[1])
    flag = jnp.where(face == 2, flags[2], flag)
    flag = jnp.where(face == 3, flags[3], flag)
    return jnp.where(c == (r ^ jnp.where(flag == 1, mask, 0)), 1.0, 0.0).astype(BF16)


def back_part(orient_ref, own_ref, near_ref, mz_ref, e_ref, s, bx, by):
    codes = [orient_ref[0, f] for f in range(4)]
    face = lax.broadcasted_iota(jnp.int32, (32, 128), 1) // 32
    own2 = own_ref.reshape(256, 128)
    near2 = near_ref.reshape(256, 128)
    mz = pltpu.roll(mz_ref[...].reshape(128, 128), lax.rem(128 - s * 64, 128), 1)
    zh, zlo = split(jnp.transpose(mz)[:64])
    perm = turned(128, 5, 31, [c % 2 for c in codes])
    mats = (
        (own2, zh, zlo),
        (near2, bdot(zh, perm).astype(BF16), bdot(zlo, perm).astype(BF16)),
    )
    cols = []
    for data, mh, ml in mats:
        for h in range(2):
            per = []
            for c in range(3):
                v = rows(data, h * 128 + c, 32, 4)
                wide = jnp.concatenate(
                    [jnp.where(face == f, v, 0.0) for f in range(4)], axis=0
                )
                wh, wl = split(wide)
                per.append(bdot(mh, wh) + (bdot(ml, wh) + bdot(mh, wl)))
            cols.append(jnp.concatenate(per, axis=0))
    ch, cl = split(jnp.concatenate(cols, axis=1))
    eh, el = split(e_ref[...])
    perm = turned(256, 5, 159, [c // 2 for c in codes])
    eh = jnp.concatenate([eh, (-bdot(perm, eh)).astype(BF16)], axis=0)
    el = jnp.concatenate([el, (-bdot(perm, el)).astype(BF16)], axis=0)
    back = bdot(ch, eh) + (bdot(ch, el) + bdot(cl, eh))
    for c in range(3):
        r = back[c * 64 : c * 64 + 64]
        bx[0, c] = r[:, :128]
        bx[1, c] = r[:, 128:256]
        col = r[:, 256:]
        by[c] = jnp.transpose(jnp.concatenate([col, col], axis=0))


def last_kernel(
    sizes_ref, cpl, orient_ref, data, xm_ref, own_ref, near_ref, mz_ref, mx_ref, my_ref, out,
    xl, cs, e_ref, bx, by,
):
    i = pl.program_id(0)
    sx, sy = sizes_ref[0, 0], sizes_ref[0, 1]

    @pl.when(i == 0)
    def _():
        active = (lax.broadcasted_iota(jnp.int32, (64, 64), 0) < sx) & (
            lax.broadcasted_iota(jnp.int32, (64, 64), 1) < sx
        )
        h0, l0 = split(jnp.where(active, xm_ref[0], 0.0))
        h1, l1 = split(jnp.where(active, xm_ref[1], 0.0))
        hi = jnp.concatenate([h0, h1], axis=1)
        xl[:64, :128] = hi
        xl[:64, 128:] = hi
        xl[64:, :128] = jnp.concatenate([l0, l1], axis=1)
        xl[64:, 128:] = jnp.zeros((64, 128), BF16)
        for c in range(3):
            for d in range(3):
                cs[c * 3 + d : c * 3 + d + 1, :] = jnp.broadcast_to(
                    cpl[c : c + 1, d : d + 1], (1, 256)
                )
        face_rows(sizes_ref, mx_ref, my_ref, e_ref)
        back_part(orient_ref, own_ref, near_ref, mz_ref, e_ref, lax.axis_index("slab"), bx, by)

    row = lax.broadcasted_iota(jnp.int32, (64, 128), 0)
    lane = lax.broadcasted_iota(jnp.int32, (64, 128), 1)
    first_x = row == 0
    last_x = row == sx - 1
    first_y = lane == 0
    last_y = lane == sy - 1
    cols = [pltpu.roll(by[c], lax.rem(128 - i * 8, 128), 1) for c in range(3)]
    for pair in range(4):
        inner = []
        for d in range(3):
            tops, lows = [], []
            for n in range(2):
                k = pair * 2 + n
                top, low = split(jnp.concatenate([data[0, d, k], data[1, d, k]], axis=0))
                tops.append(top)
                lows.append(low)
            w = jnp.concatenate(
                [jnp.concatenate(tops, axis=1), jnp.concatenate(lows, axis=1)], axis=0
            )
            r = bdot(xl[...], w)
            inner.append(r[:64] + r[64:])
        for c in range(3):
            at = c * 3
            mix = cs[at : at + 1, :] * inner[0] + cs[at + 1 : at + 2, :] * inner[1]
            mix = mix + cs[at + 2 : at + 3, :] * inner[2]
            for n in range(2):
                k = pair * 2 + n
                v = mix[:, n * 128 : n * 128 + 128]
                zrow = pl.ds(i * 8 + k, 1)
                v = v + jnp.where(first_x, bx[0, c, zrow, :], 0.0)
                v = v + jnp.where(last_x, bx[1, c, zrow, :], 0.0)
                v = v + jnp.where(first_y, cols[c][:64, k : k + 1], 0.0)
                v = v + jnp.where(last_y, cols[c][64:, k : k + 1], 0.0)
                out[k, c] = v


def first_spread(sizes, cpl, orient, data, xm, own, near, mz, mx, my):
    smem = pl.BlockSpec(memory_space=pltpu.SMEM)
    whole = lambda *shape: pl.BlockSpec(shape, lambda i: (0,) * len(shape))
    return pl.pallas_call(
        last_kernel,
        grid=(8,),
        out_shape=jax.ShapeDtypeStruct((1, 64, 3, 64, 128), F32),
        in_specs=[
            smem,
            whole(None, 3, 3),
            smem,
            pl.BlockSpec((2, 3, 8, 64, 128), lambda i: (0, 0, i, 0, 0)),
            whole(None, 2, 64, 64),
            whole(2, 32, 4, 128),
            whole(2, 32, 4, 128),
            whole(None, 4, 32, 128),
            whole(None, 2, 64, 128),
            whole(None, 2, 64, 64),
        ],
        out_specs=pl.BlockSpec((None, 8, 3, 64, 128), lambda i: (0, i, 0, 0, 0)),
        scratch_shapes=[
            pltpu.VMEM((128, 256), BF16),
            pltpu.VMEM((16, 256), F32),
            pltpu.VMEM((256, 384), F32),
            pltpu.VMEM((2, 3, 64, 128), F32),
            pltpu.VMEM((3, 128, 128), F32),
        ],
        compiler_params=pltpu.CompilerParams(vmem_limit_bytes=60 * 2**20),
        name="first_spread",
    )(sizes, cpl, orient, data, xm, own, near, mz, mx, my)


def per_device(
    field, xmats, ymats, zmats, coupling, mortar_z, mortar_x, mortar_y, matching, orient, sizes
):
    field = field.reshape(1, 64, 3, 64, 1, 128)
    own, near, mid = front(sizes, matching, field, zmats, ymats, mortar_z, mortar_x, mortar_y)
    return first_spread(
        sizes, coupling, orient, mid.reshape(2, 3, 64, 64, 128), xmats, own, near, mortar_z, mortar_x, mortar_y
    )


def solution(mesh):
    in_specs = (
        P("patch", "slab", None, None, None),
        P("patch", None, None, None),
        P("patch", None, None, None),
        P("patch", None, None, None),
        P("patch", None, None),
        P("patch", None, None, None),
        P("patch", None, None, None),
        P("patch", None, None, None),
        P("patch", None),
        P("patch", None),
        P("patch", None),
    )
    return jax.shard_map(
        per_device,
        mesh=mesh,
        in_specs=in_specs,
        out_specs=P("patch", "slab", None, None, None),
        check_vma=False,
    )
```

```python
import functools

import jax
import jax.numpy as jnp
from jax import lax
from jax.experimental import pallas as pl
from jax.experimental.pallas import tpu as pltpu
from jax.sharding import PartitionSpec as P

MESH = pl.DeviceIdType.MESH
F32 = jnp.float32
BF16 = jnp.bfloat16
MAT = (((1,), (0,)), ((), ()))
NT = (((1,), (1,)), ((), ()))


def split(a):
    hi = a.astype(BF16)
    return hi, (a - hi.astype(F32)).astype(BF16)


def bdot(a, b, dims=MAT):
    return lax.dot_general(a, b, dims, preferred_element_type=F32)


def dot3(a, b, dims=MAT):
    ah, al = split(a)
    bh, bl = split(b)
    return bdot(ah, bh, dims) + (bdot(ah, bl, dims) + bdot(al, bh, dims))


def rows(ref, start, count, stride):
    return ref[pl.ds(start, count, stride=stride), :]


def face_rows(sizes_ref, mx_ref, my_ref, e_ref):
    e_ref[...] = jnp.zeros((256, 384), F32)
    lane = lax.broadcasted_iota(jnp.int32, (32, 128), 1)
    lane64 = lax.broadcasted_iota(jnp.int32, (32, 64), 1)
    zero = jnp.zeros((32, 64), F32)
    for h in range(2):
        for f in range(2):
            at = h * 128 + f * 32
            j = h * 32
            e_ref[at : at + 32, f * 128 : f * 128 + 128] = jnp.where(
                lane < sizes_ref[0, 1], mx_ref[f, j : j + 32], 0.0
            )
            e = jnp.where(lane64 < sizes_ref[0, 0], my_ref[f, j : j + 32], 0.0)
            e_ref[at + 64 : at + 96, 256:384] = jnp.concatenate(
                [e, zero] if f == 0 else [zero, e], axis=1
            )


def trace_part(sizes_ref, block, t_ref):
    sx, sy = sizes_ref[0, 0], sizes_ref[0, 1]
    lane = lax.broadcasted_iota(jnp.int32, (64, 128), 1)
    for d in range(3):

        def body(x, accs):
            low, high = accs
            v = pltpu.roll(block[d, x], x, 1)
            low = jnp.where(lane == x, v, low)
            high = jnp.where(lane == lax.rem(x + sy - 1, 128), v, high)
            return low, high

        zero = jnp.zeros((64, 128), F32)
        low, high = lax.fori_loop(0, 64, body, (zero, zero), unroll=8)
        high = pltpu.roll(high, lax.rem(193 - sy, 128), 1)
        at = d * 64
        t_ref[at : at + 64, 0:128] = block[d, 0]
        t_ref[at : at + 64, 128:256] = block[d, jnp.maximum(sx - 1, 0)]
        t_ref[at : at + 64, 256:384] = jnp.where(lane < 64, low, high)


def mortar_part(t_ref, s, mz_ref, e_ref):
    along = dot3(t_ref[...], e_ref[...], NT)
    mz = pltpu.roll(mz_ref[...].reshape(128, 128), lax.rem(128 - s * 64, 128), 1)[:, :64]
    face = lax.broadcasted_iota(jnp.int32, (32, 256), 1) % 128 // 32
    parts = []
    for d in range(3):
        full = dot3(mz, along[d * 64 : d * 64 + 64])
        out = jnp.where(face == 0, full[:32], full[32:64])
        out = jnp.where(face == 2, full[64:96], out)
        parts.append(jnp.where(face == 3, full[96:], out))
    return parts


def zy_weights(sizes_ref, s, zm_ref, ym_ref, zl, yw):
    z_rows = [zm_ref[m, pl.ds(pl.multiple_of(s * 64, 64), 64), :] for m in range(2)]
    az = pltpu.roll(jnp.concatenate(z_rows, axis=0), lax.rem(128 - s * 64, 128), 1)
    hi, lo = split(az)
    zl[:128, :128] = hi
    zl[:128, 128:] = hi
    zl[128:, :128] = lo
    zl[128:, 128:] = jnp.zeros_like(lo)
    zero = jnp.zeros((128, 128), BF16)
    sy = sizes_ref[0, 1]
    active = (lax.broadcasted_iota(jnp.int32, (128, 128), 0) < sy) & (
        lax.broadcasted_iota(jnp.int32, (128, 128), 1) < sy
    )
    for k, m in ((0, 1), (256, 0), (512, 1)):
        hi, lo = split(jnp.transpose(jnp.where(active, ym_ref[m], 0.0)))
        yw[k : k + 128, :128] = hi
        yw[k : k + 128, 128:] = lo
        yw[k + 128 : k + 256, :128] = hi
        yw[k + 128 : k + 256, 128:] = zero


def zy_chunk(k, own, other, zl, yw, tb, out):
    for pair in range(12):
        tops, lows = [], []
        for n in (2 * pair, 2 * pair + 1):
            at = (n // 8, n % 8 + k * 8)
            top, low = split(
                jnp.concatenate([own[at], other[at]], axis=0)
            )
            tops.append(top)
            lows.append(low)
        w = jnp.concatenate(
            [jnp.concatenate(tops, axis=1), jnp.concatenate(lows, axis=1)], axis=0
        )
        r = bdot(zl[...], w)
        t = r[:128] + r[128:]
        for n in range(2):
            at = (2 * pair + n) * 64
            sh, sl = split(t[:64, n * 128 : n * 128 + 128])
            mh, ml = split(t[64:, n * 128 : n * 128 + 128])
            tb[at : at + 64, 0:128] = mh
            tb[at : at + 64, 128:256] = ml
            tb[at : at + 64, 256:384] = sh
            tb[at : at + 64, 384:512] = sl
    for d in range(3):
        at = d * 512
        a = bdot(tb[at : at + 512, :256], yw[:256])
        out[0, d] = (a[:, :128] + a[:, 128:]).reshape(8, 64, 128)
        b = bdot(tb[at : at + 512, :], yw[256:])
        out[1, d] = (b[:, :128] + b[:, 128:]).reshape(8, 64, 128)


def front_kernel(
    sizes_ref, match_ref, field, zm, ym, mz, mx, my, own_ref, near_ref, mid,
    block, other, zm_ref, ym_ref, mz_ref, mx_ref, my_ref, e_ref, t_ref, zl, yw, tb, stage,
    part, got, mine, gath, sendb, mt, mts,
    lsem, wsem, osem, fsem, psem, asem, bsem, csem, dsem,
):
    p = lax.axis_index("patch")
    s = lax.axis_index("slab")
    z, y, x = p // 16, p // 4 % 4, p % 4
    me = z * 4 + x

    def dev(a, yy):
        return ((a >> 2) * 16 + yy * 4 + (a & 3), s)

    partner = (p, 1 - s)

    def copy(src, dst, sem, k, where):
        return pltpu.make_async_remote_copy(
            src, dst, sem.at[0, k], sem.at[1, k], device_id=where, device_id_type=MESH
        )

    barrier = pltpu.get_barrier_semaphore()

    def greet(d, c):
        pl.semaphore_signal(
            barrier, inc=1, device_id=dev((me + d) & 31, y), device_id_type=MESH
        )
        return c

    pl.semaphore_signal(barrier, inc=1, device_id=partner, device_id_type=MESH)
    lax.fori_loop(1, 32, greet, 0)

    def greet_y(d, c):
        pl.semaphore_signal(
            barrier, inc=1, device_id=dev(me, (y + d) % 4), device_id_type=MESH
        )
        return c

    lax.fori_loop(1, 4, greet_y, 0)

    smalls = [
        pltpu.make_async_copy(a.at[0], b, wsem.at[n])
        for n, (a, b) in enumerate(
            ((mz, mz_ref), (mx, mx_ref), (my, my_ref), (zm, zm_ref), (ym, ym_ref))
        )
    ]
    for c in smalls:
        c.start()
    for d in range(3):

        def load_row(x, c):
            pltpu.make_async_copy(
                field.at[0, :, d, x, 0], block.at[d, x], lsem.at[d]
            ).start()
            return c

        lax.fori_loop(0, 64, load_row, 0, unroll=4)
    for c in smalls[:3]:
        c.wait()
    face_rows(sizes_ref, mx_ref, my_ref, e_ref)
    lane1 = lax.broadcasted_iota(jnp.int32, (1, 128), 1)
    row = jnp.where(lane1 == 0, match_ref[0, 0], match_ref[0, 1])
    row = jnp.where(lane1 == 2, match_ref[0, 2], row)
    row = jnp.where(lane1 == 3, match_ref[0, 3], row)
    q = row >> 2
    mt[me] = ((((q >> 2) & 3) * 32 + (q >> 4) * 4 + (q & 3)) << 2) + (row & 3)
    for d in range(3):
        pltpu.make_async_copy(block.at[d], block.at[d], lsem.at[d]).wait()
    trace_part(sizes_ref, block, t_ref)
    parts = mortar_part(t_ref, s, mz_ref, e_ref)
    half = s == 0
    for d in range(3):
        part[d] = jnp.where(half, parts[d][:, 128:], parts[d][:, :128])
    for d in range(3):
        mine[:, d, :] = jnp.where(half, parts[d][:, :128], parts[d][:, 128:])
    mine[:, 3, :] = jnp.zeros((32, 128), F32)
    pl.semaphore_wait(barrier, 35)
    c0 = copy(part, got, psem, 0, partner)
    c0.start()

    def field_start(k, c):
        for d in range(3):
            for n in range(8):
                x = k * 8 + n
                copy(field.at[0, :, d, x, 0], other.at[d, x], fsem, k, partner).start()
        return c

    def field_wait(k):
        at = other.at[:, pl.ds(pl.multiple_of(k * 8, 8), 8)]
        copy(at, at, fsem, k, partner).wait()

    def match_copy(d):
        return copy(mt.at[me], mt.at[me], asem, d, dev((me + d) & 31, y))

    def start_match(d, c):
        match_copy(d).start()
        return c

    lax.fori_loop(1, 32, start_match, 0)
    field_start(0, 0)


    def mid_start(k):
        for m in range(2):
            for d in range(3):
                for n in range(8):
                    pltpu.make_async_copy(
                        stage.at[k % 2, m, d, n], mid.at[m, d, :, k * 8 + n, 0], osem.at[k % 2]
                    ).start()

    def mid_wait(k):
        pltpu.make_async_copy(stage.at[k % 2], stage.at[k % 2], osem.at[k % 2]).wait()

    def chunks(lo, hi):
        def one(k, c):
            field_wait(k)

            @pl.when(k >= 2)
            def _():
                mid_wait(k - 2)

            zy_chunk(k, block, other, zl, yw, tb, stage.at[k % 2])
            mid_start(k)
            return c

        lax.fori_loop(lo, hi, one, 0)

    c0.wait()
    for d in range(3):
        mine[:, d, :] = mine[:, d, :] + got[d]

    def spread_copy(d):
        a = (me + d) & 31
        return copy(mine.at[a], gath.at[y * 32 + me], bsem, d, dev(a, y))

    def start_spread(d, c):
        spread_copy(d).start()
        return c

    lax.fori_loop(1, 32, start_spread, 0)
    lax.fori_loop(1, 8, field_start, 0)
    cm = copy(mine, own_ref.at[s], psem, 1, partner)
    cm.start()
    own_ref[s] = mine[...]
    gath[y * 32 + me] = mine[me]

    def wait_match(d, c):
        match_copy(d).wait()
        return c

    lax.fori_loop(1, 32, wait_match, 0)
    tos = pltpu.make_async_copy(mt, mts, lsem.at[3])
    tos.start()
    for c in smalls[3:]:
        c.wait()
    zy_weights(sizes_ref, s, zm_ref, ym_ref, zl, yw)
    chunks(0, CUTS[1])

    def wait_spread(d, c):
        spread_copy(d).wait()
        return c

    lax.fori_loop(1, 32, wait_spread, 0)

    def line_copy(d):
        at = gath.at[pl.ds(pl.multiple_of(y * 32, 32), 32)]
        return copy(at, at, csem, d, dev(me, (y + d) % 4))

    for d in range(1, 4):
        line_copy(d).start()
    tos.wait()
    chunks(CUTS[1], CUTS[2])
    for d in range(1, 4):
        line_copy(d).wait()

    lane4 = lax.broadcasted_iota(jnp.int32, (4, 128), 1) // 32

    def pick(d, c):
        a = (me + d) & 31
        out = jnp.zeros((4, 128), F32)
        for f in range(4):
            m = mts[a, 0, f]
            v = pltpu.roll(gath[m >> 2], ((f - m) & 3) * 32, 1)
            out = jnp.where(lane4 == f, v, out)
        sendb[a] = out
        return c

    def back_copy(d):
        a = (me + d) & 31
        return copy(sendb.at[a], near_ref.at[s, me], dsem, d, dev(a, y))

    def start_back(d, c):
        back_copy(d).start()
        return c

    lax.fori_loop(1, 17, pick, 0, unroll=8)
    lax.fori_loop(17, 33, pick, 0, unroll=8)
    lax.fori_loop(1, 32, start_back, 0)
    near_ref[s, me] = sendb[me]
    chunks(CUTS[2], 8)

    def wait_back(d, c):
        back_copy(d).wait()
        return c

    lax.fori_loop(1, 32, wait_back, 0)
    cn = copy(near_ref.at[s], near_ref.at[s], psem, 2, partner)
    cn.start()
    cm.wait()
    mid_wait(6)
    mid_wait(7)
    cn.wait()


CUTS = (0, 3, 6)


def front(sizes, matching, field, zm, ym, mz, mx, my):
    vmem = pl.BlockSpec(memory_space=pltpu.VMEM)
    smem = pl.BlockSpec(memory_space=pltpu.SMEM)
    hbm = pl.BlockSpec(memory_space=pl.ANY)
    dma = pltpu.SemaphoreType.DMA
    shape = jax.ShapeDtypeStruct((2, 32, 4, 128), F32)
    return pl.pallas_call(
        front_kernel,
        out_shape=(shape, shape, jax.ShapeDtypeStruct((2, 3, 64, 64, 1, 128), F32)),
        in_specs=[smem, smem] + [hbm] * 6,
        out_specs=(vmem, vmem, hbm),
        scratch_shapes=[
            pltpu.VMEM((3, 64, 64, 128), F32),
            pltpu.VMEM((3, 64, 64, 128), F32),
            pltpu.VMEM((2, 128, 128), F32),
            pltpu.VMEM((2, 128, 128), F32),
            pltpu.VMEM((4, 32, 128), F32),
            pltpu.VMEM((2, 64, 128), F32),
            pltpu.VMEM((2, 64, 64), F32),
            pltpu.VMEM((256, 384), F32),
            pltpu.VMEM((192, 384), F32),
            pltpu.VMEM((256, 256), BF16),
            pltpu.VMEM((768, 256), BF16),
            pltpu.VMEM((1536, 512), BF16),
            pltpu.VMEM((2, 2, 3, 8, 64, 128), F32),
            pltpu.VMEM((3, 32, 128), F32),
            pltpu.VMEM((3, 32, 128), F32),
            pltpu.VMEM((32, 4, 128), F32),
            pltpu.VMEM((128, 4, 128), F32),
            pltpu.VMEM((32, 4, 128), F32),
            pltpu.VMEM((32, 1, 128), jnp.int32),
            pltpu.SMEM((32, 1, 128), jnp.int32),
            dma((4,)), dma((5,)), dma((2,)), dma((2, 8)), dma((2, 3)),
            dma((2, 32)), dma((2, 32)), dma((2, 4)), dma((2, 32)),
        ],
        compiler_params=pltpu.CompilerParams(
            collective_id=0, has_side_effects=True, vmem_limit_bytes=60 * 2**20
        ),
        name="front",
    )(sizes, matching, field, zm, ym, mz, mx, my)


def turned(size, low, mask, flags):
    r = lax.broadcasted_iota(jnp.int32, (size, size), 0)
    c = lax.broadcasted_iota(jnp.int32, (size, size), 1)
    face = r // 32 % 4
    flag = jnp.where(face == 0, flags[0], flags[1])
    flag = jnp.where(face == 2, flags[2], flag)
    flag = jnp.where(face == 3, flags[3], flag)
    return jnp.where(c == (r ^ jnp.where(flag == 1, mask, 0)), 1.0, 0.0).astype(BF16)


def back_part(orient_ref, own_ref, near_ref, mz_ref, e_ref, s, bx, by):
    codes = [orient_ref[0, f] for f in range(4)]
    face = lax.broadcasted_iota(jnp.int32, (32, 128), 1) // 32
    own2 = own_ref.reshape(256, 128)
    near2 = near_ref.reshape(256, 128)
    mz = pltpu.roll(mz_ref[...].reshape(128, 128), lax.rem(128 - s * 64, 128), 1)
    zh, zlo = split(jnp.transpose(mz)[:64])
    perm = turned(128, 5, 31, [c % 2 for c in codes])
    mats = (
        (own2, zh, zlo),
        (near2, bdot(zh, perm).astype(BF16), bdot(zlo, perm).astype(BF16)),
    )
    cols = []
    for data, mh, ml in mats:
        for h in range(2):
            per = []
            for c in range(3):
                v = rows(data, h * 128 + c, 32, 4)
                wide = jnp.concatenate(
                    [jnp.where(face == f, v, 0.0) for f in range(4)], axis=0
                )
                wh, wl = split(wide)
                per.append(bdot(mh, wh) + (bdot(ml, wh) + bdot(mh, wl)))
            cols.append(jnp.concatenate(per, axis=0))
    ch, cl = split(jnp.concatenate(cols, axis=1))
    eh, el = split(e_ref[...])
    perm = turned(256, 5, 159, [c // 2 for c in codes])
    eh = jnp.concatenate([eh, (-bdot(perm, eh)).astype(BF16)], axis=0)
    el = jnp.concatenate([el, (-bdot(perm, el)).astype(BF16)], axis=0)
    back = bdot(ch, eh) + (bdot(ch, el) + bdot(cl, eh))
    for c in range(3):
        r = back[c * 64 : c * 64 + 64]
        bx[0, c] = r[:, :128]
        bx[1, c] = r[:, 128:256]
        col = r[:, 256:]
        by[c] = jnp.transpose(jnp.concatenate([col, col], axis=0))


def last_kernel(
    sizes_ref, cpl, orient_ref, data, xm_ref, own_ref, near_ref, mz_ref, mx_ref, my_ref, out,
    xl, cs, e_ref, bx, by,
):
    i = pl.program_id(0)
    sx, sy = sizes_ref[0, 0], sizes_ref[0, 1]

    @pl.when(i == 0)
    def _():
        active = (lax.broadcasted_iota(jnp.int32, (64, 64), 0) < sx) & (
            lax.broadcasted_iota(jnp.int32, (64, 64), 1) < sx
        )
        h0, l0 = split(jnp.where(active, xm_ref[0], 0.0))
        h1, l1 = split(jnp.where(active, xm_ref[1], 0.0))
        hi = jnp.concatenate([h0, h1], axis=1)
        xl[:64, :128] = hi
        xl[:64, 128:] = hi
        xl[64:, :128] = jnp.concatenate([l0, l1], axis=1)
        xl[64:, 128:] = jnp.zeros((64, 128), BF16)
        for c in range(3):
            for d in range(3):
                cs[c * 3 + d : c * 3 + d + 1, :] = jnp.broadcast_to(
                    cpl[c, :, d : d + 1], (1, 256)
                )
        face_rows(sizes_ref, mx_ref, my_ref, e_ref)
        back_part(orient_ref, own_ref, near_ref, mz_ref, e_ref, lax.axis_index("slab"), bx, by)

    lane = lax.broadcasted_iota(jnp.int32, (64, 128), 1)
    last_x = pl.ds(jnp.maximum(sx - 1, 0), 1)
    first_y = lane == 0
    last_y = lane == sy - 1
    cols = [pltpu.roll(by[c], lax.rem(128 - i * 8, 128), 1) for c in range(3)]
    for pair in range(4):
        inner = []
        for d in range(3):
            tops, lows = [], []
            for n in range(2):
                k = pair * 2 + n
                top, low = split(jnp.concatenate([data[0, d, k], data[1, d, k]], axis=0))
                tops.append(top)
                lows.append(low)
            w = jnp.concatenate(
                [jnp.concatenate(tops, axis=1), jnp.concatenate(lows, axis=1)], axis=0
            )
            r = bdot(xl[...], w)
            inner.append(r[:64] + r[64:])
        for c in range(3):
            at = c * 3
            mix = cs[at : at + 1, :] * inner[0] + cs[at + 1 : at + 2, :] * inner[1]
            mix = mix + cs[at + 2 : at + 3, :] * inner[2]
            for n in range(2):
                k = pair * 2 + n
                v = mix[:, n * 128 : n * 128 + 128]
                zrow = pl.ds(i * 8 + k, 1)
                edge = jnp.where(last_y, cols[c][64:, k : k + 1], 0.0)
                out[k, c] = v + jnp.where(first_y, cols[c][:64, k : k + 1], edge)
                out[k, c, :1, :] = out[k, c, :1, :] + bx[0, c, zrow, :]
                out[k, c, last_x, :] = out[k, c, last_x, :] + bx[1, c, zrow, :]


def first_spread(sizes, cpl, orient, data, xm, own, near, mz, mx, my):
    smem = pl.BlockSpec(memory_space=pltpu.SMEM)
    whole = lambda *shape: pl.BlockSpec(shape, lambda i: (0,) * len(shape))
    return pl.pallas_call(
        last_kernel,
        grid=(8,),
        out_shape=jax.ShapeDtypeStruct((1, 64, 3, 64, 128), F32),
        in_specs=[
            smem,
            whole(3, 1, 3),
            smem,
            pl.BlockSpec((2, 3, 8, 64, 128), lambda i: (0, 0, i, 0, 0)),
            whole(None, 2, 64, 64),
            whole(2, 32, 4, 128),
            whole(2, 32, 4, 128),
            whole(None, 4, 32, 128),
            whole(None, 2, 64, 128),
            whole(None, 2, 64, 64),
        ],
        out_specs=pl.BlockSpec((None, 8, 3, 64, 128), lambda i: (0, i, 0, 0, 0)),
        scratch_shapes=[
            pltpu.VMEM((128, 256), BF16),
            pltpu.VMEM((16, 256), F32),
            pltpu.VMEM((256, 384), F32),
            pltpu.VMEM((2, 3, 64, 128), F32),
            pltpu.VMEM((3, 128, 128), F32),
        ],
        compiler_params=pltpu.CompilerParams(vmem_limit_bytes=60 * 2**20),
        name="first_spread",
    )(sizes, cpl, orient, data, xm, own, near, mz, mx, my)


def per_device(
    field, xmats, ymats, zmats, coupling, mortar_z, mortar_x, mortar_y, matching, orient, sizes
):
    field = field.reshape(1, 64, 3, 64, 1, 128)
    own, near, mid = front(sizes, matching, field, zmats, ymats, mortar_z, mortar_x, mortar_y)
    return first_spread(
        sizes, coupling.transpose(1, 0, 2), orient, mid.reshape(2, 3, 64, 64, 128), xmats, own, near, mortar_z, mortar_x, mortar_y
    )


def solution(mesh):
    in_specs = (
        P("patch", "slab", None, None, None),
        P("patch", None, None, None),
        P("patch", None, None, None),
        P("patch", None, None, None),
        P("patch", None, None),
        P("patch", None, None, None),
        P("patch", None, None, None),
        P("patch", None, None, None),
        P("patch", None),
        P("patch", None),
        P("patch", None),
    )
    return jax.shard_map(
        per_device,
        mesh=mesh,
        in_specs=in_specs,
        out_specs=P("patch", "slab", None, None, None),
        check_vma=False,
    )
```
